32 devices in a mesh: row: 4 (over y, x), col: 8 (over z, core).
Axes of the slice: x: 2, y: 2, z: 4, core: 2. Of those that a mesh axis runs over, the one named last changes fastest.
Arguments:
- tokens: bfloat16 [8192, 4096], P(('row', 'col')), may hold values from -6 to 6
- grad_out: bfloat16 [8192, 512], P(('row', 'col')), may hold values from -0.375 to 0.375
- residual: bfloat16 [32, 2048, 1024], P(('row', 'col')), may hold values from -6 to 6
- momentum: float32 [2048, 1024], P(('row', 'col')), may hold values from -4 to 4
- kept_blocks: int32 [4, 8, 5, 128], P('row', 'col'), may hold values from 0 to 2047, as said below
- kept_counts: int32 [4, 8, 5], P('row', 'col'), may hold values from 1 to 128, as said below
Outputs:
- residual_out: bfloat16 [32, 2048, 1024], P(('row', 'col'))
- momentum_out: float32 [2048, 1024], P(('row', 'col'))
The draws below stay inside these ranges and needn't reach their ends.
Inputs may be any that keep to these rules, and one draw needn't show every extreme that they name: `kept_blocks`: valid entries of one list are distinct. Lists of section t are equal on all replicas that share row and col // 2 ** (t + 1) for t < 3, and on all replicas that share row // 2 ** (u + 1) for section 3 + u. Padding entries are arbitrary block numbers. `kept_counts`: equal within each section's group as for the lists; the largest is reached in every draw.
All inputs are finite; a program needn't handle non-finite values.
Results may differ from the reference program's by a relative error of at most 0.001.
Values sent between devices are 32-bit elements; how exact they have to be, the bound alone decides.
A program may use at most 128 MiB of HBM per device.

```python
import jax
import jax.numpy as jnp
from jax import lax

DIN = 4096
DOUT = 512
BLOCK = 1024
CAP = 128
TOK_DEV = 256
REPLICAS = 32
NBLK = 2048
COL_SECTIONS = 3
SECTIONS = 5
N_ROW = 4
N_COL = 8


def make_lists(key):
    base_order = jax.random.permutation(jax.random.fold_in(key, 11), NBLK).astype(jnp.int32)
    row_ids = jnp.arange(N_ROW, dtype=jnp.int32)[:, None]
    col_ids = jnp.arange(N_COL, dtype=jnp.int32)[None, :]
    group_total = N_ROW * N_COL
    slot_ids = jnp.arange(CAP, dtype=jnp.int32)
    list_stack = []
    count_stack = []
    for section_id in range(SECTIONS):
        if section_id < COL_SECTIONS:
            group_ids = row_ids * N_COL + col_ids // 2 ** (section_id + 1)
        else:
            group_ids = row_ids // 2 ** (section_id - COL_SECTIONS + 1) + 0 * col_ids
        section_key = jax.random.fold_in(key, 100 + section_id)
        replaced = jax.random.randint(jax.random.fold_in(section_key, 1), (group_total, CAP), 0, 16) == 0
        offsets = jax.random.randint(jax.random.fold_in(section_key, 2), (group_total, CAP), 1, NBLK // CAP)
        spare = base_order[slot_ids[None, :] + CAP * offsets]
        chosen = jnp.where(replaced, spare, base_order[:CAP][None, :])
        group_counts = jax.random.randint(jax.random.fold_in(section_key, 3), (group_total,), CAP * 3 // 4, CAP + 1)
        group_counts = group_counts.at[0].set(CAP)
        filler = jax.random.randint(jax.random.fold_in(section_key, 4), (group_total, CAP), 0, NBLK)
        chosen = jnp.where(slot_ids[None, :] < group_counts[:, None], chosen, filler)
        list_stack.append(chosen[group_ids])
        count_stack.append(group_counts[group_ids])
    return (jnp.stack(list_stack, axis=2).astype(jnp.int32), jnp.stack(count_stack, axis=2).astype(jnp.int32))


def draw_kept_blocks(key, part):
    return make_lists(key)[0]


def draw_kept_counts(key, part):
    return make_lists(key)[1]


def shard_levels(stream_key, dims, pieces, low, high):
    factor_of = 1.0
    for position, blocks in pieces:
        heights = jax.random.uniform(jax.random.fold_in(jax.random.fold_in(stream_key, 6), position), (blocks,), jnp.float32, low / len(pieces), high / len(pieces))
        factor_of = factor_of * jnp.repeat(jnp.exp(heights), dims[position] // blocks).reshape((-1,) + (1,) * (len(dims) - 1 - position))
    return factor_of


def centred(own_key, dims, scale, limit, shards=(), kind=jnp.bfloat16):
    entries = scale * jax.random.normal(own_key, dims, jnp.float32)
    if shards:
        entries = entries * shard_levels(own_key, dims, shards, -0.22, 0.18)
    return jnp.clip(entries, -limit, limit).astype(kind)


def setup_inputs(seed: int = 0) -> dict:
    keys = jax.random.split(jax.random.key(seed), 7)
    return {
        "tokens": centred(keys[0], (REPLICAS * TOK_DEV, DIN), 1.0, 6.0, ((0, 32),)),
        "grad_out": centred(keys[1], (REPLICAS * TOK_DEV, DOUT), TOK_DEV ** -0.5, 0.375, ((0, 32),)),
        "residual": centred(keys[2], (REPLICAS, NBLK, BLOCK), 1.0, 6.0, ((0, 32),)),
        "momentum": centred(keys[3], (NBLK, BLOCK), 0.5, 4.0, ((0, 32),), jnp.float32),
        "kept_blocks": draw_kept_blocks(jax.random.fold_in(keys[6], 71), 0),
        "kept_counts": draw_kept_counts(jax.random.fold_in(keys[6], 71), 0),
    }


decay_rate = 0.9


def reference(tokens, grad_out, residual, momentum, kept_blocks, kept_counts):
    replica_count = N_ROW * N_COL
    token_rows = tokens.reshape(replica_count, TOK_DEV, DIN)
    cotangents = grad_out.reshape(replica_count, TOK_DEV, DOUT)
    all_lists = kept_blocks.reshape(replica_count, SECTIONS, CAP)
    all_counts = kept_counts.reshape(replica_count, SECTIONS)
    slot_ids = jnp.arange(CAP, dtype=jnp.int32)

    def one_replica(total_sum, device_item):
        token_part, cotangent, old_residual, block_lists, block_counts = device_item
        weight_grad = lax.dot_general(token_part, cotangent, (((0,), (0,)), ((), ())), preferred_element_type=jnp.float32)
        accumulated = weight_grad.reshape(NBLK, BLOCK) + old_residual.astype(jnp.float32)
        is_valid = slot_ids[None, :] < block_counts[:, None]
        marked = jnp.where(is_valid, block_lists, NBLK).astype(jnp.int32)
        kept_mask = jnp.ones((NBLK,), jnp.float32)
        for section_id in range(SECTIONS):
            member = jnp.zeros((NBLK,), jnp.float32).at[marked[section_id]].set(1.0, mode="drop")
            kept_mask = kept_mask * member
        total_sum = total_sum + accumulated * kept_mask[:, None]
        new_residual = (accumulated * (1.0 - kept_mask)[:, None]).astype(jnp.bfloat16)
        return total_sum, new_residual

    start_sum = jnp.zeros((NBLK, BLOCK), jnp.float32)
    total_sum, residual_out = lax.scan(one_replica, start_sum, (token_rows, cotangents, residual, all_lists, all_counts))
    momentum_out = decay_rate * momentum + total_sum / replica_count
    return residual_out, momentum_out
```

```python
import functools

import jax
import jax.numpy as jnp
from jax import lax
from jax.experimental import pallas as pl
from jax.experimental.pallas import tpu as pltpu
from jax.sharding import PartitionSpec as P

decay_rate = 0.9
MESH = pl.DeviceIdType.MESH
LANES = 128


def column_of(row):
    n = row.shape[1]
    down = lax.broadcasted_iota(jnp.int32, (n, n), 0)
    along = lax.broadcasted_iota(jnp.int32, (n, n), 1)
    spread = jnp.broadcast_to(row, (n, n))
    return jnp.sum(jnp.where(down == along, spread, 0), axis=1, keepdims=True)


def local_kernel(steps, last_ref, tokens_ref, grad_ref, residual_ref, lists_ref, counts_ref,
                 out_ref, packed_ref, acc, marks, gathered):
    step = pl.program_id(0)
    chunk = residual_ref.shape[0]
    sections, capacity = lists_ref.shape
    half = grad_ref.shape[1]

    @pl.when(step == 0)
    def _():
        slot_ids = lax.broadcasted_iota(jnp.int32, (1, capacity), 1)
        last = lists_ref[sections - 1:sections, :]
        kept = jnp.where(slot_ids < counts_ref[sections - 1], 1, 0)
        for section in range(sections - 1):
            row = jnp.where(slot_ids < counts_ref[section], lists_ref[section:section + 1, :], -1)
            hits = jnp.where(column_of(row) == last, 1, 0)
            kept = kept * jnp.max(hits, axis=0, keepdims=True)
        marks[...] = jnp.where(kept > 0, last, -1)

    sub = 256
    out_ids = lax.broadcasted_iota(jnp.int32, (sub, sub), 0)
    in_ids = lax.broadcasted_iota(jnp.int32, (sub, sub), 1)
    source = jnp.where(out_ids < sub // 2, 2 * out_ids, 2 * out_ids - sub + 1)
    shuffle = (source == in_ids).astype(jnp.float32).astype(jnp.bfloat16)
    pieces = 2 * chunk // sub
    for piece in range(pieces):
        part = tokens_ref[:, piece * sub:(piece + 1) * sub]
        turned = lax.dot_general(
            shuffle, part, (((1,), (1,)), ((), ())), preferred_element_type=jnp.float32
        ).astype(jnp.bfloat16)
        grads = jnp.dot(turned, grad_ref[...], preferred_element_type=jnp.float32)
        rows = slice(piece * (sub // 2), (piece + 1) * (sub // 2))
        block_ids = step * chunk + piece * (sub // 2) + lax.broadcasted_iota(
            jnp.int32, (sub // 2, capacity), 0)
        kept = jnp.max(jnp.where(block_ids == marks[...], 1, 0), axis=1, keepdims=True) > 0
        for side in range(2):
            columns = slice(side * half, (side + 1) * half)
            total = grads[side * (sub // 2):(side + 1) * (sub // 2)] + residual_ref[rows, columns].astype(jnp.float32)
            acc[pl.ds(step * chunk + piece * (sub // 2), sub // 2), columns] = total
            out_ref[rows, columns] = jnp.where(kept, 0.0, total).astype(jnp.bfloat16)

    @pl.when(step == steps - 1)
    def _():
        def fetch(slot, carry):
            gathered[pl.ds(slot, 1), :] = acc[pl.ds(last_ref[slot], 1), :]
            return carry

        lax.fori_loop(0, capacity, fetch, 0, unroll=8)
        keep = column_of(marks[...]) >= 0
        for lane in range(packed_ref.shape[0]):
            packed_ref[lane] = jnp.where(keep, gathered[:, lane * LANES:(lane + 1) * LANES], 0.0)


def local_part(tokens, grad_out, residual, lists, counts):
    token_count, features = tokens.shape
    half = grad_out.shape[1]
    blocks, width = residual.shape
    sections, capacity = lists.shape
    chunk = 256
    steps = blocks // chunk
    return pl.pallas_call(
        functools.partial(local_kernel, steps),
        grid_spec=pltpu.PrefetchScalarGridSpec(
            num_scalar_prefetch=1,
            grid=(steps,),
            in_specs=[
                pl.BlockSpec((token_count, 2 * chunk), lambda i, s: (0, i)),
                pl.BlockSpec((token_count, half), lambda i, s: (0, 0)),
                pl.BlockSpec((chunk, width), lambda i, s: (i, 0)),
                pl.BlockSpec((sections, capacity), lambda i, s: (0, 0)),
                pl.BlockSpec(memory_space=pltpu.SMEM),
            ],
            out_specs=[
                pl.BlockSpec((chunk, width), lambda i, s: (i, 0)),
                pl.BlockSpec((width // LANES, capacity, LANES), lambda i, s: (0, 0, 0)),
            ],
            scratch_shapes=[
                pltpu.VMEM((blocks, width), jnp.float32),
                pltpu.VMEM((1, capacity), jnp.int32),
                pltpu.VMEM((capacity, width), jnp.float32),
            ],
        ),
        out_shape=[
            jax.ShapeDtypeStruct((blocks, width), jnp.bfloat16),
            jax.ShapeDtypeStruct((width // LANES, capacity, LANES), jnp.float32),
        ],
        compiler_params=pltpu.CompilerParams(dimension_semantics=("arbitrary",)),
        name="local",
    )(lists[sections - 1], tokens, grad_out, residual, lists, counts)


def sum_kernel(rows, zs, packed_ref, momentum_ref, last_ref, count_ref, out_ref,
               core_in, half, row_in, part, z_in, full,
               a_send, a_recv, b_send, b_recv, c_send, c_recv,
               d_send, d_recv, e_send, e_recv, f_send, f_recv):
    row = lax.axis_index("row")
    col = lax.axis_index("col")
    z = col // 2
    core = col % 2
    other = 1 - core
    mate = (row, z * 2 + other)

    def row_peer(i):
        return (lax.rem(row + i, rows), col)

    def z_peer(i):
        return (row, lax.rem(z + i, zs) * 2 + core)

    def send(src, dst, send_sem, recv_sem, peer):
        copy = pltpu.make_async_remote_copy(
            src_ref=src, dst_ref=dst, send_sem=send_sem, recv_sem=recv_sem,
            device_id=peer, device_id_type=MESH)
        return copy

    barrier = pltpu.get_barrier_semaphore()
    pl.semaphore_signal(barrier, inc=1, device_id=mate, device_id_type=MESH)
    for i in range(1, rows):
        pl.semaphore_signal(barrier, inc=1, device_id=row_peer(i), device_id_type=MESH)
    for i in range(1, zs):
        pl.semaphore_signal(barrier, inc=1, device_id=z_peer(i), device_id_type=MESH)
    pl.semaphore_wait(barrier, rows + zs - 1)

    sent = []

    a_copies = []
    order = [k % rows for k in range(1, rows + 1)]
    for k in order:
        target = lax.rem(row + k, rows)
        copy = send(packed_ref.at[other, target], core_in.at[k], a_send.at[k], a_recv.at[k], mate)
        copy.start()
        a_copies.append(copy)
        sent.append(copy)
    b_copies = {}
    for k, arrived in zip(order, a_copies):
        arrived.wait_recv()
        target = lax.rem(row + k, rows)
        half[k] = packed_ref[core, target] + core_in[k]
        if k:
            for j in list(range(1, zs)) + [0]:
                spot = lax.rem(z + j, zs)
                copy = send(half.at[k, spot], row_in.at[k - 1, j], b_send.at[k - 1, j],
                            b_recv.at[k - 1, j], row_peer(k))
                copy.start()
                b_copies[k, j] = copy
                sent.append(copy)
    c_copies = []
    for j in list(range(1, zs)) + [0]:
        spot = lax.rem(z + j, zs)
        for k in range(1, rows):
            b_copies[k, j].wait_recv()
        total = half[0, spot]
        for k in range(1, rows):
            total = total + row_in[k - 1, j]
        part[j] = total
        if j:
            copy = send(part.at[j], z_in.at[j - 1], c_send.at[j - 1], c_recv.at[j - 1], z_peer(j))
            copy.start()
            c_copies.append(copy)
            sent.append(copy)
    for copy in c_copies:
        copy.wait_recv()
    total = part[0]
    for j in range(1, zs):
        total = total + z_in[j - 1]
    full[core, row, z] = total

    d_copies = []
    for j in range(1, zs):
        here = full.at[core, row, z]
        copy = send(here, here, d_send.at[j - 1], d_recv.at[j - 1], z_peer(j))
        copy.start()
        d_copies.append(copy)
        sent.append(copy)
    e_copies = {}
    f_copies = []
    for j in range(zs):
        spot = lax.rem(z + zs - j, zs)
        if j:
            d_copies[j - 1].wait_recv()
        here = full.at[core, row, spot]
        for k in range(1, rows):
            copy = send(here, here, e_send.at[k - 1, j], e_recv.at[k - 1, j], row_peer(k))
            copy.start()
            e_copies[k, j] = copy
            sent.append(copy)
    for k in range(rows):
        spot = lax.rem(row + rows - k, rows)
        if k:
            for j in range(zs):
                e_copies[k, j].wait_recv()
        here = full.at[core, spot]
        copy = send(here, here, f_send.at[k], f_recv.at[k], mate)
        copy.start()
        f_copies.append(copy)
        sent.append(copy)

    shard, width = momentum_ref.shape
    capacity = last_ref.shape[1]
    owner = row * (2 * zs) + col
    own_ids = owner * shard + lax.broadcasted_iota(jnp.int32, (shard, capacity), 0)
    slot_ids = lax.broadcasted_iota(jnp.int32, (shard, capacity), 1)
    picked = jnp.logical_and(own_ids == last_ref[...], slot_ids < count_ref[...])
    pick = jnp.where(picked, 1.0, 0.0).astype(jnp.bfloat16)

    for copy in f_copies:
        copy.wait_recv()
    scale = 1.0 / (rows * 2 * zs)
    piece = full.shape[3]
    per_lane = capacity // piece
    for lane in range(width // LANES):
        parts = []
        for p in range(lane * per_lane, (lane + 1) * per_lane):
            parts.append(full[p // (rows * zs), (p // zs) % rows, p % zs])
        total = jnp.concatenate(parts, axis=0) if per_lane > 1 else parts[0]
        high = total.astype(jnp.bfloat16)
        rest = total - high.astype(jnp.float32)
        middle = rest.astype(jnp.bfloat16)
        low = (rest - middle.astype(jnp.float32)).astype(jnp.bfloat16)
        rows_here = (jnp.dot(pick, high, preferred_element_type=jnp.float32)
                     + jnp.dot(pick, middle, preferred_element_type=jnp.float32)
                     + jnp.dot(pick, low, preferred_element_type=jnp.float32))
        lanes = slice(lane * LANES, (lane + 1) * LANES)
        out_ref[:, lanes] = decay_rate * momentum_ref[:, lanes] + rows_here * scale
    for copy in sent:
        copy.wait_send()


def sum_part(packed, momentum, last, count, rows, zs):
    width_lanes, capacity, _ = packed.shape
    pieces = 2 * rows * zs
    piece = width_lanes * capacity // pieces
    packed = packed.reshape(2, rows, zs, piece, LANES)
    vmem = pl.BlockSpec(memory_space=pltpu.VMEM)
    f32 = jnp.float32
    dma = pltpu.SemaphoreType.DMA
    return pl.pallas_call(
        functools.partial(sum_kernel, rows, zs),
        out_shape=jax.ShapeDtypeStruct(momentum.shape, f32),
        in_specs=[vmem] * 4,
        out_specs=vmem,
        scratch_shapes=[
            pltpu.VMEM((rows, zs, piece, LANES), f32),
            pltpu.VMEM((rows, zs, piece, LANES), f32),
            pltpu.VMEM((rows - 1, zs, piece, LANES), f32),
            pltpu.VMEM((zs, piece, LANES), f32),
            pltpu.VMEM((zs - 1, piece, LANES), f32),
            pltpu.VMEM((2, rows, zs, piece, LANES), f32),
            dma((rows,)), dma((rows,)),
            dma((rows - 1, zs)), dma((rows - 1, zs)),
            dma((zs - 1,)), dma((zs - 1,)),
            dma((zs - 1,)), dma((zs - 1,)),
            dma((rows - 1, zs)), dma((rows - 1, zs)),
            dma((rows,)), dma((rows,)),
        ],
        compiler_params=pltpu.CompilerParams(collective_id=0, has_side_effects=True),
        name="total",
    )(packed, momentum, last, count)


def body(tokens, grad_out, residual, momentum, kept_blocks, kept_counts):
    rows = lax.axis_size("row")
    zs = lax.axis_size("col") // 2
    lists = kept_blocks[0, 0]
    counts = kept_counts[0, 0]
    sections = lists.shape[0]
    residual_out, packed = local_part(tokens, grad_out, residual[0], lists, counts)
    momentum_out = sum_part(
        packed, momentum, lists[sections - 1:], counts[sections - 1:].reshape(1, 1), rows, zs)
    return (residual_out[None], momentum_out)


def solution(mesh):
    in_specs = (
        P(("row", "col"), None),
        P(("row", "col"), None),
        P(("row", "col"), None, None),
        P(("row", "col"), None),
        P("row", "col", None, None),
        P("row", "col", None),
    )
    out_specs = (P(("row", "col"), None, None), P(("row", "col"), None))
    return jax.shard_map(body, mesh=mesh, in_specs=in_specs, out_specs=out_specs, check_vma=False)
```

```python
import functools

import jax
import jax.numpy as jnp
from jax import lax
from jax.experimental import pallas as pl
from jax.experimental.pallas import tpu as pltpu
from jax.sharding import PartitionSpec as P

decay_rate = 0.9
MESH = pl.DeviceIdType.MESH
LANES = 128


def column_of(row):
    n = row.shape[1]
    down = lax.broadcasted_iota(jnp.int32, (n, n), 0)
    along = lax.broadcasted_iota(jnp.int32, (n, n), 1)
    spread = jnp.broadcast_to(row, (n, n))
    return jnp.sum(jnp.where(down == along, spread, 0), axis=1, keepdims=True)


def local_kernel(chunk, tokens_hbm, grad_hbm, residual_hbm, lists_ref, list_ids_hbm, counts_ref,
                 out_hbm, packed_ref, tokens, grad, values, acc, gathered, list_ids,
                 token_sems, value_sems, out_sems, grad_sem, list_sem):
    blocks = values.shape[0]
    half = grad.shape[1]
    sections, _, capacity = lists_ref.shape
    steps = blocks // chunk

    def spans(step):
        return slice(step * chunk, (step + 1) * chunk), slice(2 * step * chunk, 2 * (step + 1) * chunk)

    grad_copy = pltpu.make_async_copy(grad_hbm, grad, grad_sem)
    grad_copy.start()
    list_copy = pltpu.make_async_copy(list_ids_hbm, list_ids, list_sem)
    list_copy.start()
    copies = []
    for step in range(steps):
        rows, columns = spans(step)
        token_copy = pltpu.make_async_copy(tokens_hbm.at[:, columns], tokens.at[:, columns], token_sems.at[step])
        value_copy = pltpu.make_async_copy(residual_hbm.at[rows], values.at[rows], value_sems.at[step])
        token_copy.start()
        value_copy.start()
        copies.append((token_copy, value_copy))

    slot_ids = lax.broadcasted_iota(jnp.int32, (1, capacity), 1)
    last = lists_ref[sections - 1]
    kept = jnp.where(slot_ids < counts_ref[sections - 1], 1, 0)
    for section in range(sections - 1):
        row = jnp.where(slot_ids < counts_ref[section], lists_ref[section], -1)
        hits = jnp.where(column_of(row) == last, 1, 0)
        kept = kept * jnp.max(hits, axis=0, keepdims=True)
    marks = jnp.where(kept > 0, last, -1)
    keep_slot = column_of(marks) >= 0

    sub = 256
    out_ids = lax.broadcasted_iota(jnp.int32, (sub, sub), 0)
    in_ids = lax.broadcasted_iota(jnp.int32, (sub, sub), 1)
    source = jnp.where(out_ids < sub // 2, 2 * out_ids, 2 * out_ids - sub + 1)
    shuffle = (source == in_ids).astype(jnp.float32).astype(jnp.bfloat16)
    grad_copy.wait()
    out_copies = []
    for step in range(steps):
        for copy in copies[step]:
            copy.wait()
        for piece in range(2 * chunk // sub):
            start = step * chunk + piece * (sub // 2)
            rows = slice(start, start + sub // 2)
            turned = lax.dot_general(
                shuffle, tokens[:, 2 * start:2 * start + sub], (((1,), (1,)), ((), ())),
                preferred_element_type=jnp.float32,
            ).astype(jnp.bfloat16)
            grads = jnp.dot(turned, grad[...], preferred_element_type=jnp.float32)
            block_ids = start + lax.broadcasted_iota(jnp.int32, (sub // 2, capacity), 0)
            kept_row = jnp.max(jnp.where(block_ids == marks, 1, 0), axis=1, keepdims=True) > 0
            for side in range(2):
                columns = slice(side * half, (side + 1) * half)
                total = grads[side * (sub // 2):(side + 1) * (sub // 2)] + values[rows, columns].astype(jnp.float32)
                acc[rows, columns] = total
                values[rows, columns] = jnp.where(kept_row, 0.0, total).astype(jnp.bfloat16)
        rows, _ = spans(step)
        copy = pltpu.make_async_copy(values.at[rows], out_hbm.at[rows], out_sems.at[step])
        copy.start()
        out_copies.append(copy)

    list_copy.wait()

    def fetch(slot, carry):
        gathered[pl.ds(slot, 1), :] = acc[pl.ds(list_ids[sections - 1, 0, slot], 1), :]
        return carry

    lax.fori_loop(0, capacity, fetch, 0, unroll=8)
    for lane in range(packed_ref.shape[0]):
        packed_ref[lane] = jnp.where(keep_slot, gathered[:, lane * LANES:(lane + 1) * LANES], 0.0)
    for copy in out_copies:
        copy.wait()


def local_part(tokens, grad_out, residual, lists, counts):
    token_count, features = tokens.shape
    half = grad_out.shape[1]
    blocks, width = residual.shape
    sections, _, capacity = lists.shape
    chunk = 256
    steps = blocks // chunk
    hbm = pl.BlockSpec(memory_space=pl.ANY)
    dma = pltpu.SemaphoreType.DMA
    return pl.pallas_call(
        functools.partial(local_kernel, chunk),
        in_specs=[
            hbm, hbm, hbm,
            pl.BlockSpec(memory_space=pltpu.VMEM),
            hbm,
            pl.BlockSpec(memory_space=pltpu.SMEM),
        ],
        out_specs=[hbm, pl.BlockSpec(memory_space=pltpu.VMEM)],
        scratch_shapes=[
            pltpu.VMEM((token_count, features), jnp.bfloat16),
            pltpu.VMEM((token_count, half), jnp.bfloat16),
            pltpu.VMEM((blocks, width), jnp.bfloat16),
            pltpu.VMEM((blocks, width), jnp.float32),
            pltpu.VMEM((capacity, width), jnp.float32),
            pltpu.SMEM((sections, 1, capacity), jnp.int32),
            dma((steps,)), dma((steps,)), dma((steps,)), dma(()), dma(()),
        ],
        out_shape=[
            jax.ShapeDtypeStruct((blocks, width), jnp.bfloat16),
            jax.ShapeDtypeStruct((width // LANES, capacity, LANES), jnp.float32),
        ],
        name="local",
    )(tokens, grad_out, residual, lists, lists, counts)


def sum_kernel(rows, zs, shard, packed_ref, lists_ref, counts_ref, out_ref,
               own, core_in, half, row_in, part, z_in, full,
               own_sem, a_send, a_recv, b_send, b_recv, c_send, c_recv,
               d_send, d_recv, e_send, e_recv, f_send, f_recv):
    row = lax.axis_index("row")
    col = lax.axis_index("col")
    z = col // 2
    core = col % 2
    other = 1 - core
    mate = (row, z * 2 + other)

    def row_peer(k):
        return (lax.rem(row + k, rows), col)

    def z_peer(j):
        return (row, lax.rem(z + j, zs) * 2 + core)

    sent = []

    def send(src, dst, send_sem, recv_sem, peer):
        copy = pltpu.make_async_remote_copy(
            src_ref=src, dst_ref=dst, send_sem=send_sem, recv_sem=recv_sem,
            device_id=peer, device_id_type=MESH)
        copy.start()
        sent.append(copy)
        return copy

    own_copy = pltpu.make_async_copy(packed_ref.at[core], own, own_sem)
    own_copy.start()
    barrier = pltpu.get_barrier_semaphore()
    pl.semaphore_signal(barrier, inc=1, device_id=mate, device_id_type=MESH)
    for k in range(1, rows):
        pl.semaphore_signal(barrier, inc=1, device_id=row_peer(k), device_id_type=MESH)
    for j in range(1, zs):
        pl.semaphore_signal(barrier, inc=1, device_id=z_peer(j), device_id_type=MESH)
    pl.semaphore_wait(barrier, rows + zs - 1)

    order = [j % zs for j in range(1, zs + 1)]
    a_copies = {}
    for j in order:
        spot = lax.rem(z + j, zs)
        a_copies[j] = send(packed_ref.at[other, spot], core_in.at[j], a_send.at[j], a_recv.at[j], mate)
    own_copy.wait()
    b_copies = {}
    for j in order:
        a_copies[j].wait_recv()
        half[j] = own[lax.rem(z + j, zs)] + core_in[j]
        for k in range(1, rows):
            b_copies[j, k] = send(half.at[j, lax.rem(row + k, rows)], row_in.at[j, k - 1],
                                  b_send.at[j, k - 1], b_recv.at[j, k - 1], row_peer(k))
    c_copies = []
    for j in order:
        for k in range(1, rows):
            b_copies[j, k].wait_recv()
        total = half[j, row]
        for k in range(1, rows):
            total = total + row_in[j, k - 1]
        part[j] = total
        if j:
            c_copies.append(send(part.at[j], z_in.at[j - 1], c_send.at[j - 1], c_recv.at[j - 1], z_peer(j)))
    total = part[0]
    for j, copy in enumerate(c_copies):
        copy.wait_recv()
        total = total + z_in[j]
    full[core, z, row] = total

    d_copies = {}
    for j in range(1, zs):
        here = full.at[core, z, row]
        d_copies[j] = send(here, here, d_send.at[j - 1], d_recv.at[j - 1], z_peer(j))
    e_copies = {}
    f_copies = {}

    def back_to_core(j):
        for k in range(1, rows):
            e_copies[j, k].wait_recv()
        here = full.at[core, lax.rem(z + zs - j, zs)]
        f_copies[j] = send(here, here, f_send.at[j], f_recv.at[j], mate)

    for j in range(zs):
        if j:
            d_copies[j].wait_recv()
        here = full.at[core, lax.rem(z + zs - j, zs), row]
        for k in range(1, rows):
            e_copies[j, k] = send(here, here, e_send.at[j, k - 1], e_recv.at[j, k - 1], row_peer(k))
        if j >= 2:
            back_to_core(j - 2)
    for j in range(max(zs - 2, 0), zs):
        back_to_core(j)

    sections, _, capacity = lists_ref.shape
    owner = row * (2 * zs) + col
    own_ids = owner * shard + lax.broadcasted_iota(jnp.int32, (shard, capacity), 0)
    slot_ids = lax.broadcasted_iota(jnp.int32, (shard, capacity), 1)
    picked = jnp.logical_and(own_ids == lists_ref[sections - 1], slot_ids < counts_ref[sections - 1])
    pick = jnp.where(picked, 1.0, 0.0).astype(jnp.bfloat16)
    lane_groups = out_ref.shape[1] // LANES // 2
    slabs = zs // lane_groups

    def emit(side):
        for lane in range(lane_groups):
            parts = [full[side, slab, r] for slab in range(lane * slabs, (lane + 1) * slabs) for r in range(rows)]
            total = jnp.concatenate(parts, axis=0)
            high = total.astype(jnp.bfloat16)
            rest = total - high.astype(jnp.float32)
            middle = rest.astype(jnp.bfloat16)
            low = (rest - middle.astype(jnp.float32)).astype(jnp.bfloat16)
            rows_here = (jnp.dot(pick, high, preferred_element_type=jnp.float32)
                         + jnp.dot(pick, middle, preferred_element_type=jnp.float32)
                         + jnp.dot(pick, low, preferred_element_type=jnp.float32))
            lanes = pl.ds(pl.multiple_of((side * lane_groups + lane) * LANES, LANES), LANES)
            out_ref[:, lanes] = rows_here

    emit(core)
    for j in range(zs):
        f_copies[j].wait_recv()
    emit(other)
    for copy in sent:
        copy.wait_send()


def sum_part(packed, shard, lists, counts, rows, zs):
    width_lanes, capacity, _ = packed.shape
    piece = width_lanes * capacity // (2 * rows * zs)
    packed = packed.reshape(2, zs, rows, piece, LANES)
    vmem = pl.BlockSpec(memory_space=pltpu.VMEM)
    f32 = jnp.float32
    dma = pltpu.SemaphoreType.DMA
    return pl.pallas_call(
        functools.partial(sum_kernel, rows, zs, shard),
        out_shape=jax.ShapeDtypeStruct((shard, width_lanes * LANES), f32),
        in_specs=[pl.BlockSpec(memory_space=pl.ANY), vmem, pl.BlockSpec(memory_space=pltpu.SMEM)],
        out_specs=vmem,
        scratch_shapes=[
            pltpu.VMEM((zs, rows, piece, LANES), f32),
            pltpu.VMEM((zs, rows, piece, LANES), f32),
            pltpu.VMEM((zs, rows, piece, LANES), f32),
            pltpu.VMEM((zs, rows - 1, piece, LANES), f32),
            pltpu.VMEM((zs, piece, LANES), f32),
            pltpu.VMEM((zs - 1, piece, LANES), f32),
            pltpu.VMEM((2, zs, rows, piece, LANES), f32),
            dma(()),
            dma((zs,)), dma((zs,)),
            dma((zs, rows - 1)), dma((zs, rows - 1)),
            dma((zs - 1,)), dma((zs - 1,)),
            dma((zs - 1,)), dma((zs - 1,)),
            dma((zs, rows - 1)), dma((zs, rows - 1)),
            dma((zs,)), dma((zs,)),
        ],
        compiler_params=pltpu.CompilerParams(collective_id=0, has_side_effects=True),
        name="total",
    )(packed, lists, counts)


def body(tokens, grad_out, residual, momentum, kept_blocks, kept_counts):
    rows = lax.axis_size("row")
    zs = lax.axis_size("col") // 2
    sections, capacity = kept_blocks.shape[2:]
    lists = kept_blocks.reshape(sections, 1, capacity)
    counts = kept_counts.reshape(sections)
    residual_out, packed = local_part(tokens, grad_out, residual[0], lists, counts)
    total_shard = sum_part(packed, momentum.shape[0], lists, counts, rows, zs)
    momentum_out = decay_rate * momentum + total_shard / (rows * 2 * zs)
    return (residual_out[None], momentum_out)


def solution(mesh):
    in_specs = (
        P(("row", "col"), None),
        P(("row", "col"), None),
        P(("row", "col"), None, None),
        P(("row", "col"), None),
        P("row", "col", None, None),
        P("row", "col", None),
    )
    out_specs = (P(("row", "col"), None, None), P(("row", "col"), None))
    return jax.shard_map(body, mesh=mesh, in_specs=in_specs, out_specs=out_specs, check_vma=False)
```

```python
import functools

import jax
import jax.numpy as jnp
from jax import lax
from jax.experimental import pallas as pl
from jax.experimental.pallas import tpu as pltpu
from jax.sharding import PartitionSpec as P

decay_rate = 0.9
MESH = pl.DeviceIdType.MESH
LANES = 128


def column_of(row):
    n = row.shape[1]
    down = lax.broadcasted_iota(jnp.int32, (n, n), 0)
    along = lax.broadcasted_iota(jnp.int32, (n, n), 1)
    spread = jnp.broadcast_to(row, (n, n))
    return jnp.sum(jnp.where(down == along, spread, 0), axis=1, keepdims=True)


def local_kernel(chunk, tokens_hbm, grad_hbm, residual_hbm, lists_ref, list_ids_hbm, counts_ref,
                 out_hbm, packed_ref, tokens, grad, values, turned, acc, gathered, list_ids,
                 token_sems, value_sems, out_sems, grad_sem, list_sem):
    blocks = values.shape[0]
    half = grad.shape[1]
    sections, _, capacity = lists_ref.shape
    steps = blocks // chunk

    def spans(step):
        return slice(step * chunk, (step + 1) * chunk), slice(2 * step * chunk, 2 * (step + 1) * chunk)

    grad_copy = pltpu.make_async_copy(grad_hbm, grad, grad_sem)
    grad_copy.start()
    list_copy = pltpu.make_async_copy(list_ids_hbm, list_ids, list_sem)
    list_copy.start()
    token_copies = []
    value_copies = []
    for step in range(steps):
        rows, columns = spans(step)
        token_copies.append(pltpu.make_async_copy(tokens_hbm.at[:, columns], tokens.at[:, columns], token_sems.at[step]))
        value_copies.append(pltpu.make_async_copy(residual_hbm.at[rows], values.at[rows], value_sems.at[step]))
    token_copies[0].start()
    for step in range(steps):
        if step + 1 < steps:
            token_copies[step + 1].start()
        value_copies[step].start()

    slot_ids = lax.broadcasted_iota(jnp.int32, (1, capacity), 1)
    last = lists_ref[sections - 1]
    kept = jnp.where(slot_ids < counts_ref[sections - 1], 1, 0)
    for section in range(sections - 1):
        row = jnp.where(slot_ids < counts_ref[section], lists_ref[section], -1)
        hits = jnp.where(column_of(row) == last, 1, 0)
        kept = kept * jnp.max(hits, axis=0, keepdims=True)
    marks = jnp.where(kept > 0, last, -1)
    keep_slot = column_of(marks) >= 0

    sub = 256
    out_ids = lax.broadcasted_iota(jnp.int32, (sub, sub), 0)
    in_ids = lax.broadcasted_iota(jnp.int32, (sub, sub), 1)
    source = jnp.where(out_ids < sub // 2, 2 * out_ids, 2 * out_ids - sub + 1)
    shuffle = (source == in_ids).astype(jnp.float32).astype(jnp.bfloat16)
    pieces = 2 * chunk // sub
    out_copies = []

    def turn(step, piece):
        columns = slice((step * pieces + piece) * sub, (step * pieces + piece + 1) * sub)
        turned[columns, :] = lax.dot_general(
            shuffle, tokens[:, columns], (((1,), (1,)), ((), ())), preferred_element_type=jnp.float32
        ).astype(jnp.bfloat16)

    token_copies[0].wait()
    for piece in range(pieces):
        turn(0, piece)
    grad_copy.wait()
    for step in range(steps):
        value_copies[step].wait()
        if step + 1 < steps:
            token_copies[step + 1].wait()
        for piece in range(pieces):
            if step + 1 < steps:
                turn(step + 1, piece)
            start = step * chunk + piece * (sub // 2)
            rows = slice(start, start + sub // 2)
            grads = jnp.dot(turned[2 * start:2 * start + sub, :], grad[...], preferred_element_type=jnp.float32)
            block_ids = start + lax.broadcasted_iota(jnp.int32, (sub // 2, capacity), 0)
            kept_row = jnp.max(jnp.where(block_ids == marks, 1, 0), axis=1, keepdims=True) > 0
            for side in range(2):
                columns = slice(side * half, (side + 1) * half)
                total = grads[side * (sub // 2):(side + 1) * (sub // 2)] + values[rows, columns].astype(jnp.float32)
                acc[rows, columns] = total
                values[rows, columns] = jnp.where(kept_row, 0.0, total).astype(jnp.bfloat16)
        rows, _ = spans(step)
        copy = pltpu.make_async_copy(values.at[rows], out_hbm.at[rows], out_sems.at[step])
        copy.start()
        out_copies.append(copy)

    list_copy.wait()

    def fetch(slot, carry):
        gathered[pl.ds(slot, 1), :] = acc[pl.ds(list_ids[sections - 1, 0, slot], 1), :]
        return carry

    lax.fori_loop(0, capacity, fetch, 0, unroll=8)
    for lane in range(packed_ref.shape[0]):
        packed_ref[lane] = jnp.where(keep_slot, gathered[:, lane * LANES:(lane + 1) * LANES], 0.0)
    for copy in out_copies:
        copy.wait()


def local_part(tokens, grad_out, residual, lists, counts):
    token_count, features = tokens.shape
    half = grad_out.shape[1]
    blocks, width = residual.shape
    sections, _, capacity = lists.shape
    chunk = 512
    steps = blocks // chunk
    hbm = pl.BlockSpec(memory_space=pl.ANY)
    dma = pltpu.SemaphoreType.DMA
    return pl.pallas_call(
        functools.partial(local_kernel, chunk),
        in_specs=[
            hbm, hbm, hbm,
            pl.BlockSpec(memory_space=pltpu.VMEM),
            hbm,
            pl.BlockSpec(memory_space=pltpu.SMEM),
        ],
        out_specs=[hbm, pl.BlockSpec(memory_space=pltpu.VMEM)],
        scratch_shapes=[
            pltpu.VMEM((token_count, features), jnp.bfloat16),
            pltpu.VMEM((token_count, half), jnp.bfloat16),
            pltpu.VMEM((blocks, width), jnp.bfloat16),
            pltpu.VMEM((features, token_count), jnp.bfloat16),
            pltpu.VMEM((blocks, width), jnp.float32),
            pltpu.VMEM((capacity, width), jnp.float32),
            pltpu.SMEM((sections, 1, capacity), jnp.int32),
            dma((steps,)), dma((steps,)), dma((steps,)), dma(()), dma(()),
        ],
        out_shape=[
            jax.ShapeDtypeStruct((blocks, width), jnp.bfloat16),
            jax.ShapeDtypeStruct((width // LANES, capacity, LANES), jnp.float32),
        ],
        name="local",
    )(tokens, grad_out, residual, lists, lists, counts)


def sum_kernel(rows, zs, shard, packed_ref, lists_ref, counts_ref, out_ref,
               own, core_in, half, row_in, part, z_in, full,
               own_sem, a_send, a_recv, b_send, b_recv, c_send, c_recv,
               d_send, d_recv, e_send, e_recv, f_send, f_recv):
    row = lax.axis_index("row")
    col = lax.axis_index("col")
    z = col // 2
    core = col % 2
    other = 1 - core
    mate = (row, z * 2 + other)

    def row_peer(k):
        return (lax.rem(row + k, rows), col)

    def z_peer(j):
        return (row, lax.rem(z + j, zs) * 2 + core)

    sent = []

    def send(src, dst, send_sem, recv_sem, peer):
        copy = pltpu.make_async_remote_copy(
            src_ref=src, dst_ref=dst, send_sem=send_sem, recv_sem=recv_sem,
            device_id=peer, device_id_type=MESH)
        copy.start()
        sent.append(copy)
        return copy

    own_copy = pltpu.make_async_copy(packed_ref.at[core], own, own_sem)
    own_copy.start()
    barrier = pltpu.get_barrier_semaphore()
    pl.semaphore_signal(barrier, inc=1, device_id=mate, device_id_type=MESH)
    for k in range(1, rows):
        pl.semaphore_signal(barrier, inc=1, device_id=row_peer(k), device_id_type=MESH)
    for j in range(1, zs):
        pl.semaphore_signal(barrier, inc=1, device_id=z_peer(j), device_id_type=MESH)
    pl.semaphore_wait(barrier, rows + zs - 1)

    order = [j % zs for j in range(1, zs + 1)]
    a_copies = {}
    for j in order:
        spot = lax.rem(z + j, zs)
        a_copies[j] = send(packed_ref.at[other, spot], core_in.at[j], a_send.at[j], a_recv.at[j], mate)
    own_copy.wait()
    b_copies = {}
    for j in order:
        a_copies[j].wait_recv()
        half[j] = own[lax.rem(z + j, zs)] + core_in[j]
        for k in range(1, rows):
            b_copies[j, k] = send(half.at[j, lax.rem(row + k, rows)], row_in.at[j, k - 1],
                                  b_send.at[j, k - 1], b_recv.at[j, k - 1], row_peer(k))
    c_copies = []
    for j in order:
        for k in range(1, rows):
            b_copies[j, k].wait_recv()
        total = half[j, row]
        for k in range(1, rows):
            total = total + row_in[j, k - 1]
        part[j] = total
        if j:
            c_copies.append(send(part.at[j], z_in.at[j - 1], c_send.at[j - 1], c_recv.at[j - 1], z_peer(j)))
    total = part[0]
    for j, copy in enumerate(c_copies):
        copy.wait_recv()
        total = total + z_in[j]
    full[core, z, row] = total

    d_copies = {}
    for j in range(1, zs):
        here = full.at[core, z, row]
        d_copies[j] = send(here, here, d_send.at[j - 1], d_recv.at[j - 1], z_peer(j))
    e_copies = {}
    f_copies = {}

    def back_to_core(j):
        for k in range(1, rows):
            e_copies[j, k].wait_recv()
        here = full.at[core, lax.rem(z + zs - j, zs)]
        f_copies[j] = send(here, here, f_send.at[j], f_recv.at[j], mate)

    for j in range(zs):
        if j:
            d_copies[j].wait_recv()
        here = full.at[core, lax.rem(z + zs - j, zs), row]
        for k in range(1, rows):
            e_copies[j, k] = send(here, here, e_send.at[j, k - 1], e_recv.at[j, k - 1], row_peer(k))
        if j >= 2:
            back_to_core(j - 2)
    for j in range(max(zs - 2, 0), zs):
        back_to_core(j)

    sections, _, capacity = lists_ref.shape
    owner = row * (2 * zs) + col
    own_ids = owner * shard + lax.broadcasted_iota(jnp.int32, (shard, capacity), 0)
    slot_ids = lax.broadcasted_iota(jnp.int32, (shard, capacity), 1)
    picked = jnp.logical_and(own_ids == lists_ref[sections - 1], slot_ids < counts_ref[sections - 1])
    pick = jnp.where(picked, 1.0, 0.0).astype(jnp.bfloat16)
    lane_groups = out_ref.shape[1] // LANES // 2
    slabs = zs // lane_groups

    def emit(side):
        for lane in range(lane_groups):
            parts = [full[side, slab, r] for slab in range(lane * slabs, (lane + 1) * slabs) for r in range(rows)]
            total = jnp.concatenate(parts, axis=0)
            high = total.astype(jnp.bfloat16)
            rest = total - high.astype(jnp.float32)
            middle = rest.astype(jnp.bfloat16)
            low = (rest - middle.astype(jnp.float32)).astype(jnp.bfloat16)
            rows_here = (jnp.dot(pick, high, preferred_element_type=jnp.float32)
                         + jnp.dot(pick, middle, preferred_element_type=jnp.float32)
                         + jnp.dot(pick, low, preferred_element_type=jnp.float32))
            lanes = pl.ds(pl.multiple_of((side * lane_groups + lane) * LANES, LANES), LANES)
            out_ref[:, lanes] = rows_here

    emit(core)
    for j in range(zs):
        f_copies[j].wait_recv()
    emit(other)
    for copy in sent:
        copy.wait_send()


def sum_part(packed, shard, lists, counts, rows, zs):
    width_lanes, capacity, _ = packed.shape
    piece = width_lanes * capacity // (2 * rows * zs)
    packed = packed.reshape(2, zs, rows, piece, LANES)
    vmem = pl.BlockSpec(memory_space=pltpu.VMEM)
    f32 = jnp.float32
    dma = pltpu.SemaphoreType.DMA
    return pl.pallas_call(
        functools.partial(sum_kernel, rows, zs, shard),
        out_shape=jax.ShapeDtypeStruct((shard, width_lanes * LANES), f32),
        in_specs=[pl.BlockSpec(memory_space=pl.ANY), vmem, pl.BlockSpec(memory_space=pltpu.SMEM)],
        out_specs=vmem,
        scratch_shapes=[
            pltpu.VMEM((zs, rows, piece, LANES), f32),
            pltpu.VMEM((zs, rows, piece, LANES), f32),
            pltpu.VMEM((zs, rows, piece, LANES), f32),
            pltpu.VMEM((zs, rows - 1, piece, LANES), f32),
            pltpu.VMEM((zs, piece, LANES), f32),
            pltpu.VMEM((zs - 1, piece, LANES), f32),
            pltpu.VMEM((2, zs, rows, piece, LANES), f32),
            dma(()),
            dma((zs,)), dma((zs,)),
            dma((zs, rows - 1)), dma((zs, rows - 1)),
            dma((zs - 1,)), dma((zs - 1,)),
            dma((zs - 1,)), dma((zs - 1,)),
            dma((zs, rows - 1)), dma((zs, rows - 1)),
            dma((zs,)), dma((zs,)),
        ],
        compiler_params=pltpu.CompilerParams(collective_id=0, has_side_effects=True),
        name="total",
    )(packed, lists, counts)


def body(tokens, grad_out, residual, momentum, kept_blocks, kept_counts):
    rows = lax.axis_size("row")
    zs = lax.axis_size("col") // 2
    sections, capacity = kept_blocks.shape[2:]
    lists = kept_blocks.reshape(sections, 1, capacity)
    counts = kept_counts.reshape(sections)
    residual_out, packed = local_part(tokens, grad_out, residual[0], lists, counts)
    total_shard = sum_part(packed, momentum.shape[0], lists, counts, rows, zs)
    momentum_out = decay_rate * momentum + total_shard / (rows * 2 * zs)
    return (residual_out[None], momentum_out)


def solution(mesh):
    in_specs = (
        P(("row", "col"), None),
        P(("row", "col"), None),
        P(("row", "col"), None, None),
        P(("row", "col"), None),
        P("row", "col", None, None),
        P("row", "col", None),
    )
    out_specs = (P(("row", "col"), None, None), P(("row", "col"), None))
    return jax.shard_map(body, mesh=mesh, in_specs=in_specs, out_specs=out_specs, check_vma=False)
```

```python
import functools

import jax
import jax.numpy as jnp
from jax import lax
from jax.experimental import pallas as pl
from jax.experimental.pallas import tpu as pltpu
from jax.sharding import PartitionSpec as P

decay_rate = 0.9
MESH = pl.DeviceIdType.MESH
LANES = 128


def column_of(row):
    n = row.shape[1]
    down = lax.broadcasted_iota(jnp.int32, (n, n), 0)
    along = lax.broadcasted_iota(jnp.int32, (n, n), 1)
    spread = jnp.broadcast_to(row, (n, n))
    return jnp.sum(jnp.where(down == along, spread, 0), axis=1, keepdims=True)


def flipped(index, mask):
    for bit in range(mask.bit_length()):
        if mask >> bit & 1:
            index = index + 2**bit * (1 - 2 * (index // 2**bit % 2))
    return index


def local_kernel(chunk, tokens_hbm, grad_hbm, residual_hbm, lists_ref, list_ids_hbm, counts_ref,
                 out_hbm, packed_ref, tokens, grad, values, turned, acc, gathered, list_ids,
                 token_sems, value_sems, out_sems, grad_sem, list_sem):
    blocks = values.shape[0]
    half = grad.shape[1]
    sections, _, capacity = lists_ref.shape
    steps = blocks // chunk

    def spans(step):
        return slice(step * chunk, (step + 1) * chunk), slice(2 * step * chunk, 2 * (step + 1) * chunk)

    grad_copy = pltpu.make_async_copy(grad_hbm, grad, grad_sem)
    grad_copy.start()
    list_copy = pltpu.make_async_copy(list_ids_hbm, list_ids, list_sem)
    list_copy.start()
    token_copies = []
    value_copies = []
    for step in range(steps):
        rows, columns = spans(step)
        token_copies.append(pltpu.make_async_copy(tokens_hbm.at[:, columns], tokens.at[:, columns], token_sems.at[step]))
        value_copies.append(pltpu.make_async_copy(residual_hbm.at[rows], values.at[rows], value_sems.at[step]))
    token_copies[0].start()
    for step in range(steps):
        if step + 1 < steps:
            token_copies[step + 1].start()
        value_copies[step].start()

    slot_ids = lax.broadcasted_iota(jnp.int32, (1, capacity), 1)
    last = lists_ref[sections - 1]
    kept = jnp.where(slot_ids < counts_ref[sections - 1], 1, 0)
    for section in range(sections - 1):
        row = jnp.where(slot_ids < counts_ref[section], lists_ref[section], -1)
        hits = jnp.where(column_of(row) == last, 1, 0)
        kept = kept * jnp.max(hits, axis=0, keepdims=True)
    marks = jnp.where(kept > 0, last, -1)
    keep_slot = column_of(marks) >= 0

    sub = 256
    out_ids = lax.broadcasted_iota(jnp.int32, (sub, sub), 0)
    in_ids = lax.broadcasted_iota(jnp.int32, (sub, sub), 1)
    source = jnp.where(out_ids < sub // 2, 2 * out_ids, 2 * out_ids - sub + 1)
    shuffle = (source == in_ids).astype(jnp.float32).astype(jnp.bfloat16)
    pieces = 2 * chunk // sub
    out_copies = []

    def turn(step, piece):
        columns = slice((step * pieces + piece) * sub, (step * pieces + piece + 1) * sub)
        turned[columns, :] = lax.dot_general(
            shuffle, tokens[:, columns], (((1,), (1,)), ((), ())), preferred_element_type=jnp.float32
        ).astype(jnp.bfloat16)

    token_copies[0].wait()
    for piece in range(pieces):
        turn(0, piece)
    grad_copy.wait()
    for step in range(steps):
        value_copies[step].wait()
        if step + 1 < steps:
            token_copies[step + 1].wait()
        for piece in range(pieces):
            if step + 1 < steps:
                turn(step + 1, piece)
            start = step * chunk + piece * (sub // 2)
            rows = slice(start, start + sub // 2)
            grads = jnp.dot(turned[2 * start:2 * start + sub, :], grad[...], preferred_element_type=jnp.float32)
            block_ids = start + lax.broadcasted_iota(jnp.int32, (sub // 2, capacity), 0)
            kept_row = jnp.max(jnp.where(block_ids == marks, 1, 0), axis=1, keepdims=True) > 0
            for side in range(2):
                columns = slice(side * half, (side + 1) * half)
                total = grads[side * (sub // 2):(side + 1) * (sub // 2)] + values[rows, columns].astype(jnp.float32)
                acc[rows, columns] = total
                values[rows, columns] = jnp.where(kept_row, 0.0, total).astype(jnp.bfloat16)
        rows, _ = spans(step)
        copy = pltpu.make_async_copy(values.at[rows], out_hbm.at[rows], out_sems.at[step])
        copy.start()
        out_copies.append(copy)

    list_copy.wait()

    def fetch(slot, carry):
        gathered[pl.ds(slot, 1), :] = acc[pl.ds(list_ids[sections - 1, 0, slot], 1), :]
        return carry

    lax.fori_loop(0, capacity, fetch, 0, unroll=8)
    for lane in range(packed_ref.shape[0]):
        packed_ref[lane] = jnp.where(keep_slot, gathered[:, lane * LANES:(lane + 1) * LANES], 0.0)
    for copy in out_copies:
        copy.wait()


def local_part(tokens, grad_out, residual, lists, counts):
    token_count, features = tokens.shape
    half = grad_out.shape[1]
    blocks, width = residual.shape
    sections, _, capacity = lists.shape
    chunk = 512
    steps = blocks // chunk
    hbm = pl.BlockSpec(memory_space=pl.ANY)
    dma = pltpu.SemaphoreType.DMA
    return pl.pallas_call(
        functools.partial(local_kernel, chunk),
        in_specs=[
            hbm, hbm, hbm,
            pl.BlockSpec(memory_space=pltpu.VMEM),
            hbm,
            pl.BlockSpec(memory_space=pltpu.SMEM),
        ],
        out_specs=[hbm, pl.BlockSpec(memory_space=pltpu.VMEM)],
        scratch_shapes=[
            pltpu.VMEM((token_count, features), jnp.bfloat16),
            pltpu.VMEM((token_count, half), jnp.bfloat16),
            pltpu.VMEM((blocks, width), jnp.bfloat16),
            pltpu.VMEM((features, token_count), jnp.bfloat16),
            pltpu.VMEM((blocks, width), jnp.float32),
            pltpu.VMEM((capacity, width), jnp.float32),
            pltpu.SMEM((sections, 1, capacity), jnp.int32),
            dma((steps,)), dma((steps,)), dma((steps,)), dma(()), dma(()),
        ],
        out_shape=[
            jax.ShapeDtypeStruct((blocks, width), jnp.bfloat16),
            pltpu.VMEM((width // LANES, capacity, LANES), jnp.float32),
        ],
        name="local",
    )(tokens, grad_out, residual, lists, lists, counts)


def sum_kernel(rows, zs, shard, packed_ref, lists_ref, counts_ref, out_ref,
               own, core_in, half, row_in, part, z_in, full,
               own_sem, a_send, a_recv, b_send, b_recv, c_send, c_recv,
               d_send, d_recv, e_send, e_recv, f_send, f_recv):
    row = lax.axis_index("row")
    col = lax.axis_index("col")
    z = col // 2
    core = col % 2
    other = 1 - core
    mate = (row, z * 2 + other)

    def row_peer(k):
        return (flipped(row, k), col)

    def z_peer(j):
        return (row, flipped(z, j) * 2 + core)

    sent = []

    def send(src, dst, send_sem, recv_sem, peer):
        copy = pltpu.make_async_remote_copy(
            src_ref=src, dst_ref=dst, send_sem=send_sem, recv_sem=recv_sem,
            device_id=peer, device_id_type=MESH)
        copy.start()
        sent.append(copy)
        return copy

    own_copy = pltpu.make_async_copy(packed_ref.at[core], own, own_sem)
    own_copy.start()
    barrier = pltpu.get_barrier_semaphore()
    pl.semaphore_signal(barrier, inc=1, device_id=mate, device_id_type=MESH)
    for k in range(1, rows):
        pl.semaphore_signal(barrier, inc=1, device_id=row_peer(k), device_id_type=MESH)
    for j in range(1, zs):
        pl.semaphore_signal(barrier, inc=1, device_id=z_peer(j), device_id_type=MESH)
    pl.semaphore_wait(barrier, rows + zs - 1)

    order = list(range(zs - 1, -1, -1))
    far_rows = list(range(rows - 1, 0, -1))
    a_copies = {}
    for j in order:
        spot = flipped(z, j)
        a_copies[j] = send(packed_ref.at[other, spot], core_in.at[j], a_send.at[j], a_recv.at[j], mate)
    own_copy.wait()
    b_copies = {}
    for j in order:
        a_copies[j].wait_recv()
        half[j] = own[flipped(z, j)] + core_in[j]
        for k in far_rows:
            b_copies[j, k] = send(half.at[j, flipped(row, k)], row_in.at[j, k - 1],
                                  b_send.at[j, k - 1], b_recv.at[j, k - 1], row_peer(k))
    c_copies = {}
    for j in order:
        for k in range(1, rows):
            b_copies[j, k].wait_recv()
        total = half[j, row]
        for k in range(1, rows):
            total = total + row_in[j, k - 1]
        part[j] = total
        if j:
            c_copies[j] = send(part.at[j], z_in.at[j - 1], c_send.at[j - 1], c_recv.at[j - 1], z_peer(j))
    total = part[0]
    for j in range(1, zs):
        c_copies[j].wait_recv()
        total = total + z_in[j - 1]
    full[core, z, row] = total

    sections, _, capacity = lists_ref.shape
    owner = row * (2 * zs) + col
    own_ids = owner * shard + lax.broadcasted_iota(jnp.int32, (shard, capacity), 0)
    slot_ids = lax.broadcasted_iota(jnp.int32, (shard, capacity), 1)
    picked = jnp.logical_and(own_ids == lists_ref[sections - 1], slot_ids < counts_ref[sections - 1])
    pick = jnp.where(picked, 1.0, 0.0).astype(jnp.bfloat16)
    lane_groups = out_ref.shape[1] // LANES // 2
    slabs = zs // lane_groups

    def emit_lane(side, lane):
        parts = [full[side, lane * slabs + slab, r] for slab in range(slabs) for r in range(rows)]
        total = jnp.concatenate(parts, axis=0)
        high = total.astype(jnp.bfloat16)
        rest = total - high.astype(jnp.float32)
        middle = rest.astype(jnp.bfloat16)
        low = (rest - middle.astype(jnp.float32)).astype(jnp.bfloat16)
        rows_here = (jnp.dot(pick, high, preferred_element_type=jnp.float32)
                     + jnp.dot(pick, middle, preferred_element_type=jnp.float32)
                     + jnp.dot(pick, low, preferred_element_type=jnp.float32))
        out_ref[:, pl.ds(pl.multiple_of((side * lane_groups + lane) * LANES, LANES), LANES)] = rows_here

    d_copies = {}
    for j in order[:-1]:
        here = full.at[core, z, row]
        d_copies[j] = send(here, here, d_send.at[j - 1], d_recv.at[j - 1], z_peer(j))
    e_copies = {}
    f_copies = {}

    def back_to_core(j):
        for k in range(1, rows):
            e_copies[j, k].wait_recv()
        here = full.at[core, flipped(z, j)]
        f_copies[j] = send(here, here, f_send.at[j], f_recv.at[j], mate)

    for j in range(zs):
        if j:
            d_copies[j].wait_recv()
        here = full.at[core, flipped(z, j), row]
        for k in far_rows:
            e_copies[j, k] = send(here, here, e_send.at[j, k - 1], e_recv.at[j, k - 1], row_peer(k))
        if j >= 2:
            back_to_core(j - 2)
    for j in range(max(zs - 2, 0), zs):
        back_to_core(j)

    if slabs == 1:
        for j in range(zs):
            emit_lane(core, flipped(z, j))
        for j in range(zs):
            f_copies[j].wait_recv()
            emit_lane(other, flipped(z, j))
    else:
        for lane in range(lane_groups):
            emit_lane(core, lane)
        for j in range(zs):
            f_copies[j].wait_recv()
        for lane in range(lane_groups):
            emit_lane(other, lane)
    for copy in sent:
        copy.wait_send()


def sum_part(packed, shard, lists, counts, rows, zs):
    width_lanes, capacity, _ = packed.shape
    piece = width_lanes * capacity // (2 * rows * zs)
    packed = packed.reshape(2, zs, rows, piece, LANES)
    vmem = pl.BlockSpec(memory_space=pltpu.VMEM)
    f32 = jnp.float32
    dma = pltpu.SemaphoreType.DMA
    return pl.pallas_call(
        functools.partial(sum_kernel, rows, zs, shard),
        out_shape=pltpu.VMEM((shard, width_lanes * LANES), f32),
        in_specs=[pl.BlockSpec(memory_space=pl.ANY), vmem, pl.BlockSpec(memory_space=pltpu.SMEM)],
        out_specs=vmem,
        scratch_shapes=[
            pltpu.VMEM((zs, rows, piece, LANES), f32),
            pltpu.VMEM((zs, rows, piece, LANES), f32),
            pltpu.VMEM((zs, rows, piece, LANES), f32),
            pltpu.VMEM((zs, rows - 1, piece, LANES), f32),
            pltpu.VMEM((zs, piece, LANES), f32),
            pltpu.VMEM((zs - 1, piece, LANES), f32),
            pltpu.VMEM((2, zs, rows, piece, LANES), f32),
            dma(()),
            dma((zs,)), dma((zs,)),
            dma((zs, rows - 1)), dma((zs, rows - 1)),
            dma((zs - 1,)), dma((zs - 1,)),
            dma((zs - 1,)), dma((zs - 1,)),
            dma((zs, rows - 1)), dma((zs, rows - 1)),
            dma((zs,)), dma((zs,)),
        ],
        compiler_params=pltpu.CompilerParams(collective_id=0, has_side_effects=True),
        name="total",
    )(packed, lists, counts)


def body(tokens, grad_out, residual, momentum, kept_blocks, kept_counts):
    rows = lax.axis_size("row")
    zs = lax.axis_size("col") // 2
    sections, capacity = kept_blocks.shape[2:]
    lists = kept_blocks.reshape(sections, 1, capacity)
    counts = kept_counts.reshape(sections)
    residual_out, packed = local_part(tokens, grad_out, residual[0], lists, counts)
    total_shard = sum_part(packed, momentum.shape[0], lists, counts, rows, zs)
    momentum_out = decay_rate * momentum + total_shard / (rows * 2 * zs)
    return (residual_out[None], momentum_out)


def solution(mesh):
    in_specs = (
        P(("row", "col"), None),
        P(("row", "col"), None),
        P(("row", "col"), None, None),
        P(("row", "col"), None),
        P("row", "col", None, None),
        P("row", "col", None),
    )
    out_specs = (P(("row", "col"), None, None), P(("row", "col"), None))
    return jax.shard_map(body, mesh=mesh, in_specs=in_specs, out_specs=out_specs, check_vma=False)
```

```python
import functools

import jax
import jax.numpy as jnp
from jax import lax
from jax.experimental import pallas as pl
from jax.experimental.pallas import tpu as pltpu
from jax.sharding import PartitionSpec as P

decay_rate = 0.9
MESH = pl.DeviceIdType.MESH
LANES = 128


def column_of(row):
    n = row.shape[1]
    down = lax.broadcasted_iota(jnp.int32, (n, n), 0)
    along = lax.broadcasted_iota(jnp.int32, (n, n), 1)
    spread = jnp.broadcast_to(row, (n, n))
    return jnp.sum(jnp.where(down == along, spread, 0), axis=1, keepdims=True)


def flipped(index, mask):
    for bit in range(mask.bit_length()):
        if mask >> bit & 1:
            index = index + 2**bit * (1 - 2 * (index // 2**bit % 2))
    return index


def local_kernel(chunk, tokens_hbm, grad_hbm, residual_hbm, lists_ref, list_ids_hbm, counts_ref,
                 out_hbm, packed_ref, tokens, grad, values, turned, acc, gathered, list_ids,
                 token_sems, value_sems, out_sems, grad_sem, list_sem):
    blocks = values.shape[0]
    half = grad.shape[1]
    sections, _, capacity = lists_ref.shape
    steps = blocks // chunk

    def spans(step):
        return slice(step * chunk, (step + 1) * chunk), slice(2 * step * chunk, 2 * (step + 1) * chunk)

    grad_copy = pltpu.make_async_copy(grad_hbm, grad, grad_sem)
    grad_copy.start()
    list_copy = pltpu.make_async_copy(list_ids_hbm, list_ids, list_sem)
    list_copy.start()
    token_copies = []
    value_copies = []
    for step in range(steps):
        rows, columns = spans(step)
        token_copies.append(pltpu.make_async_copy(tokens_hbm.at[:, columns], tokens.at[:, columns], token_sems.at[step]))
        value_copies.append(pltpu.make_async_copy(residual_hbm.at[rows], values.at[rows], value_sems.at[step]))
    token_copies[0].start()
    for step in range(steps):
        if step + 1 < steps:
            token_copies[step + 1].start()
        value_copies[step].start()

    slot_ids = lax.broadcasted_iota(jnp.int32, (1, capacity), 1)
    last = lists_ref[sections - 1]
    kept = jnp.where(slot_ids < counts_ref[sections - 1], 1, 0)
    for section in range(sections - 1):
        row = jnp.where(slot_ids < counts_ref[section], lists_ref[section], -1)
        hits = jnp.where(column_of(row) == last, 1, 0)
        kept = kept * jnp.max(hits, axis=0, keepdims=True)
    marks = jnp.where(kept > 0, last, -1)
    keep_slot = column_of(marks) >= 0

    sub = 256
    out_ids = lax.broadcasted_iota(jnp.int32, (sub, sub), 0)
    in_ids = lax.broadcasted_iota(jnp.int32, (sub, sub), 1)
    source = jnp.where(out_ids < sub // 2, 2 * out_ids, 2 * out_ids - sub + 1)
    shuffle = (source == in_ids).astype(jnp.float32).astype(jnp.bfloat16)
    pieces = 2 * chunk // sub
    out_copies = []

    def turn(step, piece):
        columns = slice((step * pieces + piece) * sub, (step * pieces + piece + 1) * sub)
        turned[columns, :] = lax.dot_general(
            shuffle, tokens[:, columns], (((1,), (1,)), ((), ())), preferred_element_type=jnp.float32
        ).astype(jnp.bfloat16)

    token_copies[0].wait()
    for piece in range(pieces):
        turn(0, piece)
    grad_copy.wait()
    for step in range(steps):
        value_copies[step].wait()
        if step + 1 < steps:
            token_copies[step + 1].wait()
        for piece in range(pieces):
            if step + 1 < steps:
                turn(step + 1, piece)
            start = step * chunk + piece * (sub // 2)
            rows = slice(start, start + sub // 2)
            grads = jnp.dot(turned[2 * start:2 * start + sub, :], grad[...], preferred_element_type=jnp.float32)
            block_ids = start + lax.broadcasted_iota(jnp.int32, (sub // 2, capacity), 0)
            kept_row = jnp.max(jnp.where(block_ids == marks, 1, 0), axis=1, keepdims=True) > 0
            for side in range(2):
                columns = slice(side * half, (side + 1) * half)
                total = grads[side * (sub // 2):(side + 1) * (sub // 2)] + values[rows, columns].astype(jnp.float32)
                acc[rows, columns] = total
                values[rows, columns] = jnp.where(kept_row, 0.0, total).astype(jnp.bfloat16)
        rows, _ = spans(step)
        copy = pltpu.make_async_copy(values.at[rows], out_hbm.at[rows], out_sems.at[step])
        copy.start()
        out_copies.append(copy)

    list_copy.wait()

    def fetch(slot, carry):
        gathered[pl.ds(slot, 1), :] = acc[pl.ds(list_ids[sections - 1, 0, slot], 1), :]
        return carry

    lax.fori_loop(0, capacity, fetch, 0, unroll=8)
    for lane in range(packed_ref.shape[0]):
        packed_ref[lane] = jnp.where(keep_slot, gathered[:, lane * LANES:(lane + 1) * LANES], 0.0)
    for copy in out_copies:
        copy.wait()


def local_part(tokens, grad_out, residual, lists, counts):
    token_count, features = tokens.shape
    half = grad_out.shape[1]
    blocks, width = residual.shape
    sections, _, capacity = lists.shape
    chunk = 512
    steps = blocks // chunk
    hbm = pl.BlockSpec(memory_space=pl.ANY)
    dma = pltpu.SemaphoreType.DMA
    return pl.pallas_call(
        functools.partial(local_kernel, chunk),
        in_specs=[
            hbm, hbm, hbm,
            pl.BlockSpec(memory_space=pltpu.VMEM),
            hbm,
            pl.BlockSpec(memory_space=pltpu.SMEM),
        ],
        out_specs=[hbm, pl.BlockSpec(memory_space=pltpu.VMEM)],
        scratch_shapes=[
            pltpu.VMEM((token_count, features), jnp.bfloat16),
            pltpu.VMEM((token_count, half), jnp.bfloat16),
            pltpu.VMEM((blocks, width), jnp.bfloat16),
            pltpu.VMEM((features, token_count), jnp.bfloat16),
            pltpu.VMEM((blocks, width), jnp.float32),
            pltpu.VMEM((capacity, width), jnp.float32),
            pltpu.SMEM((sections, 1, capacity), jnp.int32),
            dma((steps,)), dma((steps,)), dma((steps,)), dma(()), dma(()),
        ],
        out_shape=[
            jax.ShapeDtypeStruct((blocks, width), jnp.bfloat16),
            pltpu.VMEM((width // LANES, capacity, LANES), jnp.float32),
        ],
        name="local",
    )(tokens, grad_out, residual, lists, lists, counts)


def sum_kernel(rows, zs, shard, packed_ref, lists_ref, counts_ref, out_ref,
               core_in, half, row_in, part, z_in, full,
               a_send, a_recv, b_send, b_recv, c_send, c_recv,
               d_send, d_recv, e_send, e_recv, f_send, f_recv):
    row = lax.axis_index("row")
    col = lax.axis_index("col")
    z = col // 2
    core = col % 2
    other = 1 - core
    mate = (row, z * 2 + other)

    def row_peer(k):
        return (flipped(row, k), col)

    def z_peer(j):
        return (row, flipped(z, j) * 2 + core)

    sent = []

    def send(src, dst, send_sem, recv_sem, peer):
        copy = pltpu.make_async_remote_copy(
            src_ref=src, dst_ref=dst, send_sem=send_sem, recv_sem=recv_sem,
            device_id=peer, device_id_type=MESH)
        copy.start()
        sent.append(copy)
        return copy

    barrier = pltpu.get_barrier_semaphore()
    pl.semaphore_signal(barrier, inc=1, device_id=mate, device_id_type=MESH)
    for k in range(1, rows):
        pl.semaphore_signal(barrier, inc=1, device_id=row_peer(k), device_id_type=MESH)
    for j in range(1, zs):
        pl.semaphore_signal(barrier, inc=1, device_id=z_peer(j), device_id_type=MESH)
    pl.semaphore_wait(barrier, rows + zs - 1)

    order = list(range(zs - 1, -1, -1))
    far_rows = list(range(rows - 1, 0, -1))
    a_copies = {}
    for j in order:
        spot = flipped(z, j)
        a_copies[j] = send(packed_ref.at[other, spot], core_in.at[j], a_send.at[j], a_recv.at[j], mate)
    b_copies = {}
    for j in order:
        a_copies[j].wait_recv()
        half[j] = packed_ref[core, flipped(z, j)] + core_in[j]
        for k in far_rows:
            b_copies[j, k] = send(half.at[j, flipped(row, k)], row_in.at[j, k - 1],
                                  b_send.at[j, k - 1], b_recv.at[j, k - 1], row_peer(k))
    c_copies = {}
    for j in order:
        for k in range(1, rows):
            b_copies[j, k].wait_recv()
        total = half[j, row]
        for k in range(1, rows):
            total = total + row_in[j, k - 1]
        part[j] = total
        if j:
            c_copies[j] = send(part.at[j], z_in.at[j - 1], c_send.at[j - 1], c_recv.at[j - 1], z_peer(j))
    total = part[0]
    for j in range(1, zs):
        c_copies[j].wait_recv()
        total = total + z_in[j - 1]
    full[core, z, row] = total

    sections, _, capacity = lists_ref.shape
    owner = row * (2 * zs) + col
    own_ids = owner * shard + lax.broadcasted_iota(jnp.int32, (shard, capacity), 0)
    slot_ids = lax.broadcasted_iota(jnp.int32, (shard, capacity), 1)
    picked = jnp.logical_and(own_ids == lists_ref[sections - 1], slot_ids < counts_ref[sections - 1])
    pick = jnp.where(picked, 1.0, 0.0).astype(jnp.bfloat16)
    lane_groups = out_ref.shape[1] // LANES // 2
    slabs = zs // lane_groups

    def emit_lane(side, lane):
        parts = [full[side, lane * slabs + slab, r] for slab in range(slabs) for r in range(rows)]
        total = jnp.concatenate(parts, axis=0)
        high = total.astype(jnp.bfloat16)
        rest = total - high.astype(jnp.float32)
        middle = rest.astype(jnp.bfloat16)
        low = (rest - middle.astype(jnp.float32)).astype(jnp.bfloat16)
        rows_here = (jnp.dot(pick, high, preferred_element_type=jnp.float32)
                     + jnp.dot(pick, middle, preferred_element_type=jnp.float32)
                     + jnp.dot(pick, low, preferred_element_type=jnp.float32))
        out_ref[:, pl.ds(pl.multiple_of((side * lane_groups + lane) * LANES, LANES), LANES)] = rows_here

    d_copies = {}
    for j in order[:-1]:
        here = full.at[core, z, row]
        d_copies[j] = send(here, here, d_send.at[j - 1], d_recv.at[j - 1], z_peer(j))
    e_copies = {}
    f_copies = {}

    def back_to_core(j):
        for k in range(1, rows):
            e_copies[j, k].wait_recv()
        here = full.at[core, flipped(z, j)]
        f_copies[j] = send(here, here, f_send.at[j], f_recv.at[j], mate)

    for j in range(zs):
        if j:
            d_copies[j].wait_recv()
        here = full.at[core, flipped(z, j), row]
        for k in far_rows:
            e_copies[j, k] = send(here, here, e_send.at[j, k - 1], e_recv.at[j, k - 1], row_peer(k))
        if j >= 2:
            back_to_core(j - 2)
    for j in range(max(zs - 2, 0), zs):
        back_to_core(j)

    if slabs == 1:
        for j in range(zs):
            emit_lane(core, flipped(z, j))
        for j in range(zs):
            f_copies[j].wait_recv()
            emit_lane(other, flipped(z, j))
    else:
        for lane in range(lane_groups):
            emit_lane(core, lane)
        for j in range(zs):
            f_copies[j].wait_recv()
        for lane in range(lane_groups):
            emit_lane(other, lane)
    for copy in sent:
        copy.wait_send()


def sum_part(packed, shard, lists, counts, rows, zs):
    width_lanes, capacity, _ = packed.shape
    piece = width_lanes * capacity // (2 * rows * zs)
    packed = packed.reshape(2, zs, rows, piece, LANES)
    packed = pltpu.with_memory_space_constraint(packed, pltpu.VMEM)
    vmem = pl.BlockSpec(memory_space=pltpu.VMEM)
    f32 = jnp.float32
    dma = pltpu.SemaphoreType.DMA
    return pl.pallas_call(
        functools.partial(sum_kernel, rows, zs, shard),
        out_shape=pltpu.VMEM((shard, width_lanes * LANES), f32),
        in_specs=[vmem, vmem, pl.BlockSpec(memory_space=pltpu.SMEM)],
        out_specs=vmem,
        scratch_shapes=[
            pltpu.VMEM((zs, rows, piece, LANES), f32),
            pltpu.VMEM((zs, rows, piece, LANES), f32),
            pltpu.VMEM((zs, rows - 1, piece, LANES), f32),
            pltpu.VMEM((zs, piece, LANES), f32),
            pltpu.VMEM((zs - 1, piece, LANES), f32),
            pltpu.VMEM((2, zs, rows, piece, LANES), f32),
            dma((zs,)), dma((zs,)),
            dma((zs, rows - 1)), dma((zs, rows - 1)),
            dma((zs - 1,)), dma((zs - 1,)),
            dma((zs - 1,)), dma((zs - 1,)),
            dma((zs, rows - 1)), dma((zs, rows - 1)),
            dma((zs,)), dma((zs,)),
        ],
        compiler_params=pltpu.CompilerParams(collective_id=0, has_side_effects=True),
        name="total",
    )(packed, lists, counts)


def body(tokens, grad_out, residual, momentum, kept_blocks, kept_counts):
    rows = lax.axis_size("row")
    zs = lax.axis_size("col") // 2
    sections, capacity = kept_blocks.shape[2:]
    lists = kept_blocks.reshape(sections, 1, capacity)
    counts = kept_counts.reshape(sections)
    residual_out, packed = local_part(tokens, grad_out, residual[0], lists, counts)
    total_shard = sum_part(packed, momentum.shape[0], lists, counts, rows, zs)
    momentum_out = decay_rate * momentum + total_shard / (rows * 2 * zs)
    return (residual_out[None], momentum_out)


def solution(mesh):
    in_specs = (
        P(("row", "col"), None),
        P(("row", "col"), None),
        P(("row", "col"), None, None),
        P(("row", "col"), None),
        P("row", "col", None, None),
        P("row", "col", None),
    )
    out_specs = (P(("row", "col"), None, None), P(("row", "col"), None))
    return jax.shard_map(body, mesh=mesh, in_specs=in_specs, out_specs=out_specs, check_vma=False)
```

```python
import functools

import jax
import jax.numpy as jnp
from jax import lax
from jax.experimental import pallas as pl
from jax.experimental.pallas import tpu as pltpu
from jax.sharding import PartitionSpec as P

decay_rate = 0.9
MESH = pl.DeviceIdType.MESH
LANES = 128


def column_of(row):
    n = row.shape[1]
    down = lax.broadcasted_iota(jnp.int32, (n, n), 0)
    along = lax.broadcasted_iota(jnp.int32, (n, n), 1)
    spread = jnp.broadcast_to(row, (n, n))
    return jnp.sum(jnp.where(down == along, spread, 0), axis=1, keepdims=True)


def flipped(index, mask):
    for bit in range(mask.bit_length()):
        if mask >> bit & 1:
            index = index + 2**bit * (1 - 2 * (index // 2**bit % 2))
    return index


def local_kernel(chunk, tokens_hbm, grad_hbm, residual_hbm, lists_ref, list_ids_hbm, counts_ref,
                 out_hbm, packed_ref, tokens, grad, values, turned, acc, gathered, list_ids,
                 token_sems, value_sems, out_sems, grad_sem, list_sem):
    blocks = values.shape[0]
    half = grad.shape[1]
    sections, _, capacity = lists_ref.shape
    steps = blocks // chunk

    def spans(step):
        return slice(step * chunk, (step + 1) * chunk), slice(2 * step * chunk, 2 * (step + 1) * chunk)

    grad_copy = pltpu.make_async_copy(grad_hbm, grad, grad_sem)
    grad_copy.start()
    list_copy = pltpu.make_async_copy(list_ids_hbm, list_ids, list_sem)
    list_copy.start()
    token_copies = []
    value_copies = []
    for step in range(steps):
        rows, columns = spans(step)
        token_copies.append(pltpu.make_async_copy(tokens_hbm.at[:, columns], tokens.at[:, columns], token_sems.at[step]))
        value_copies.append(pltpu.make_async_copy(residual_hbm.at[rows], values.at[rows], value_sems.at[step]))
    token_copies[0].start()
    for step in range(steps):
        if step + 1 < steps:
            token_copies[step + 1].start()
        value_copies[step].start()

    slot_ids = lax.broadcasted_iota(jnp.int32, (1, capacity), 1)
    last = lists_ref[sections - 1]
    kept = jnp.where(slot_ids < counts_ref[sections - 1], 1, 0)
    for section in range(sections - 1):
        row = jnp.where(slot_ids < counts_ref[section], lists_ref[section], -1)
        hits = jnp.where(column_of(row) == last, 1, 0)
        kept = kept * jnp.max(hits, axis=0, keepdims=True)
    marks = jnp.where(kept > 0, last, -1)
    keep_slot = column_of(marks) >= 0

    sub = 256
    out_ids = lax.broadcasted_iota(jnp.int32, (sub, sub), 0)
    in_ids = lax.broadcasted_iota(jnp.int32, (sub, sub), 1)
    source = jnp.where(out_ids < sub // 2, 2 * out_ids, 2 * out_ids - sub + 1)
    shuffle = (source == in_ids).astype(jnp.float32).astype(jnp.bfloat16)
    pieces = 2 * chunk // sub
    out_copies = []

    def turn(step, piece):
        columns = slice((step * pieces + piece) * sub, (step * pieces + piece + 1) * sub)
        turned[columns, :] = lax.dot_general(
            shuffle, tokens[:, columns], (((1,), (1,)), ((), ())), preferred_element_type=jnp.float32
        ).astype(jnp.bfloat16)

    token_copies[0].wait()
    for piece in range(pieces):
        turn(0, piece)
    grad_copy.wait()
    for step in range(steps):
        value_copies[step].wait()
        if step + 1 < steps:
            token_copies[step + 1].wait()
        for piece in range(pieces):
            if step + 1 < steps:
                turn(step + 1, piece)
            start = step * chunk + piece * (sub // 2)
            rows = slice(start, start + sub // 2)
            grads = jnp.dot(turned[2 * start:2 * start + sub, :], grad[...], preferred_element_type=jnp.float32)
            block_ids = start + lax.broadcasted_iota(jnp.int32, (sub // 2, capacity), 0)
            kept_row = jnp.max(jnp.where(block_ids == marks, 1, 0), axis=1, keepdims=True) > 0
            for side in range(2):
                columns = slice(side * half, (side + 1) * half)
                total = grads[side * (sub // 2):(side + 1) * (sub // 2)] + values[rows, columns].astype(jnp.float32)
                acc[rows, columns] = total
                values[rows, columns] = jnp.where(kept_row, 0.0, total).astype(jnp.bfloat16)
            if piece % 2 == 1:
                done = slice(start - sub // 2, start + sub // 2)
                copy = pltpu.make_async_copy(values.at[done], out_hbm.at[done], out_sems.at[len(out_copies)])
                copy.start()
                out_copies.append(copy)

    list_copy.wait()

    def fetch(slot, carry):
        gathered[pl.ds(slot, 1), :] = acc[pl.ds(list_ids[sections - 1, 0, slot], 1), :]
        return carry

    lax.fori_loop(0, capacity, fetch, 0, unroll=8)
    for lane in range(packed_ref.shape[0]):
        packed_ref[lane] = jnp.where(keep_slot, gathered[:, lane * LANES:(lane + 1) * LANES], 0.0)
    for copy in out_copies:
        copy.wait()


def local_part(tokens, grad_out, residual, lists, counts):
    token_count, features = tokens.shape
    half = grad_out.shape[1]
    blocks, width = residual.shape
    sections, _, capacity = lists.shape
    chunk = 512
    steps = blocks // chunk
    hbm = pl.BlockSpec(memory_space=pl.ANY)
    dma = pltpu.SemaphoreType.DMA
    return pl.pallas_call(
        functools.partial(local_kernel, chunk),
        in_specs=[
            hbm, hbm, hbm,
            pl.BlockSpec(memory_space=pltpu.VMEM),
            hbm,
            pl.BlockSpec(memory_space=pltpu.SMEM),
        ],
        out_specs=[hbm, pl.BlockSpec(memory_space=pltpu.VMEM)],
        scratch_shapes=[
            pltpu.VMEM((token_count, features), jnp.bfloat16),
            pltpu.VMEM((token_count, half), jnp.bfloat16),
            pltpu.VMEM((blocks, width), jnp.bfloat16),
            pltpu.VMEM((features, token_count), jnp.bfloat16),
            pltpu.VMEM((blocks, width), jnp.float32),
            pltpu.VMEM((capacity, width), jnp.float32),
            pltpu.SMEM((sections, 1, capacity), jnp.int32),
            dma((steps,)), dma((steps,)), dma((blocks // 256,)), dma(()), dma(()),
        ],
        out_shape=[
            jax.ShapeDtypeStruct((blocks, width), jnp.bfloat16),
            pltpu.VMEM((width // LANES, capacity, LANES), jnp.float32),
        ],
        name="local",
    )(tokens, grad_out, residual, lists, lists, counts)


def sum_kernel(rows, zs, shard, packed_ref, lists_ref, counts_ref, out_ref,
               core_in, half, row_in, part, z_in, full,
               a_send, a_recv, b_send, b_recv, c_send, c_recv,
               d_send, d_recv, e_send, e_recv, f_send, f_recv):
    row = lax.axis_index("row")
    col = lax.axis_index("col")
    z = col // 2
    core = col % 2
    other = 1 - core
    mate = (row, z * 2 + other)

    def row_peer(k):
        return (flipped(row, k), col)

    def z_peer(j):
        return (row, flipped(z, j) * 2 + core)

    sent = []

    def send(src, dst, send_sem, recv_sem, peer):
        copy = pltpu.make_async_remote_copy(
            src_ref=src, dst_ref=dst, send_sem=send_sem, recv_sem=recv_sem,
            device_id=peer, device_id_type=MESH)
        copy.start()
        sent.append(copy)
        return copy

    barrier = pltpu.get_barrier_semaphore()
    pl.semaphore_signal(barrier, inc=1, device_id=mate, device_id_type=MESH)
    for k in range(1, rows):
        pl.semaphore_signal(barrier, inc=1, device_id=row_peer(k), device_id_type=MESH)
    for j in range(1, zs):
        pl.semaphore_signal(barrier, inc=1, device_id=z_peer(j), device_id_type=MESH)
    pl.semaphore_wait(barrier, rows + zs - 1)

    order = list(range(zs - 1, -1, -1))
    far_rows = list(range(rows - 1, 0, -1))
    a_copies = {}
    for j in order:
        spot = flipped(z, j)
        a_copies[j] = send(packed_ref.at[other, spot], core_in.at[j], a_send.at[j], a_recv.at[j], mate)
    b_copies = {}
    for j in order:
        a_copies[j].wait_recv()
        half[j] = packed_ref[core, flipped(z, j)] + core_in[j]
        for k in far_rows:
            b_copies[j, k] = send(half.at[j, flipped(row, k)], row_in.at[j, k - 1],
                                  b_send.at[j, k - 1], b_recv.at[j, k - 1], row_peer(k))
    c_copies = {}
    for j in order:
        for k in range(1, rows):
            b_copies[j, k].wait_recv()
        total = half[j, row]
        for k in range(1, rows):
            total = total + row_in[j, k - 1]
        part[j] = total
        if j:
            c_copies[j] = send(part.at[j], z_in.at[j - 1], c_send.at[j - 1], c_recv.at[j - 1], z_peer(j))
    total = part[0]
    for j in range(1, zs):
        c_copies[j].wait_recv()
        total = total + z_in[j - 1]
    full[core, z, row] = total

    sections, _, capacity = lists_ref.shape
    owner = row * (2 * zs) + col
    own_ids = owner * shard + lax.broadcasted_iota(jnp.int32, (shard, capacity), 0)
    slot_ids = lax.broadcasted_iota(jnp.int32, (shard, capacity), 1)
    picked = jnp.logical_and(own_ids == lists_ref[sections - 1], slot_ids < counts_ref[sections - 1])
    pick = jnp.where(picked, 1.0, 0.0).astype(jnp.bfloat16)
    lane_groups = out_ref.shape[1] // LANES // 2
    slabs = zs // lane_groups

    def emit_lane(side, lane):
        parts = [full[side, lane * slabs + slab, r] for slab in range(slabs) for r in range(rows)]
        total = jnp.concatenate(parts, axis=0)
        high = total.astype(jnp.bfloat16)
        rest = total - high.astype(jnp.float32)
        middle = rest.astype(jnp.bfloat16)
        low = (rest - middle.astype(jnp.float32)).astype(jnp.bfloat16)
        rows_here = (jnp.dot(pick, high, preferred_element_type=jnp.float32)
                     + jnp.dot(pick, middle, preferred_element_type=jnp.float32)
                     + jnp.dot(pick, low, preferred_element_type=jnp.float32))
        out_ref[:, pl.ds(pl.multiple_of((side * lane_groups + lane) * LANES, LANES), LANES)] = rows_here

    d_copies = {}
    for j in order[:-1]:
        here = full.at[core, z, row]
        d_copies[j] = send(here, here, d_send.at[j - 1], d_recv.at[j - 1], z_peer(j))
    e_copies = {}
    f_copies = {}

    def back_to_core(j):
        for k in range(rows):
            if k:
                e_copies[j, k].wait_recv()
            here = full.at[core, flipped(z, j), flipped(row, k)]
            f_copies[j, k] = send(here, here, f_send.at[j, k], f_recv.at[j, k], mate)

    for j in range(zs):
        if j:
            d_copies[j].wait_recv()
        here = full.at[core, flipped(z, j), row]
        for k in far_rows:
            e_copies[j, k] = send(here, here, e_send.at[j, k - 1], e_recv.at[j, k - 1], row_peer(k))
        if j >= 2:
            back_to_core(j - 2)
    for j in range(max(zs - 2, 0), zs):
        back_to_core(j)

    if slabs == 1:
        for j in range(zs):
            emit_lane(core, flipped(z, j))
        for j in range(zs):
            for k in range(rows):
                f_copies[j, k].wait_recv()
            emit_lane(other, flipped(z, j))
    else:
        for lane in range(lane_groups):
            emit_lane(core, lane)
        for j in range(zs):
            for k in range(rows):
                f_copies[j, k].wait_recv()
        for lane in range(lane_groups):
            emit_lane(other, lane)
    for copy in sent:
        copy.wait_send()


def sum_part(packed, shard, lists, counts, rows, zs):
    width_lanes, capacity, _ = packed.shape
    piece = width_lanes * capacity // (2 * rows * zs)
    packed = packed.reshape(2, zs, rows, piece, LANES)
    packed = pltpu.with_memory_space_constraint(packed, pltpu.VMEM)
    vmem = pl.BlockSpec(memory_space=pltpu.VMEM)
    f32 = jnp.float32
    dma = pltpu.SemaphoreType.DMA
    return pl.pallas_call(
        functools.partial(sum_kernel, rows, zs, shard),
        out_shape=pltpu.VMEM((shard, width_lanes * LANES), f32),
        in_specs=[vmem, vmem, pl.BlockSpec(memory_space=pltpu.SMEM)],
        out_specs=vmem,
        scratch_shapes=[
            pltpu.VMEM((zs, rows, piece, LANES), f32),
            pltpu.VMEM((zs, rows, piece, LANES), f32),
            pltpu.VMEM((zs, rows - 1, piece, LANES), f32),
            pltpu.VMEM((zs, piece, LANES), f32),
            pltpu.VMEM((zs - 1, piece, LANES), f32),
            pltpu.VMEM((2, zs, rows, piece, LANES), f32),
            dma((zs,)), dma((zs,)),
            dma((zs, rows - 1)), dma((zs, rows - 1)),
            dma((zs - 1,)), dma((zs - 1,)),
            dma((zs - 1,)), dma((zs - 1,)),
            dma((zs, rows - 1)), dma((zs, rows - 1)),
            dma((zs, rows)), dma((zs, rows)),
        ],
        compiler_params=pltpu.CompilerParams(collective_id=0, has_side_effects=True),
        name="total",
    )(packed, lists, counts)


def body(tokens, grad_out, residual, momentum, kept_blocks, kept_counts):
    rows = lax.axis_size("row")
    zs = lax.axis_size("col") // 2
    sections, capacity = kept_blocks.shape[2:]
    lists = kept_blocks.reshape(sections, 1, capacity)
    counts = kept_counts.reshape(sections)
    residual_out, packed = local_part(tokens, grad_out, residual[0], lists, counts)
    total_shard = sum_part(packed, momentum.shape[0], lists, counts, rows, zs)
    momentum_out = decay_rate * momentum + total_shard / (rows * 2 * zs)
    return (residual_out[None], momentum_out)


def solution(mesh):
    in_specs = (
        P(("row", "col"), None),
        P(("row", "col"), None),
        P(("row", "col"), None, None),
        P(("row", "col"), None),
        P("row", "col", None, None),
        P("row", "col", None),
    )
    out_specs = (P(("row", "col"), None, None), P(("row", "col"), None))
    return jax.shard_map(body, mesh=mesh, in_specs=in_specs, out_specs=out_specs, check_vma=False)
```
